256 devices in a mesh: row: 8 (over y, core), col: 32 (over z, x).
Axes of the slice: x: 4, y: 4, z: 8, core: 2. Of those that a mesh axis runs over, the one named last changes fastest.
Arguments:
- amps: bfloat16 [1024, 256, 256], P('row', 'col'), may hold values from -6 to 6
- ints: bfloat16 [16384, 256, 256], P(('row', 'col')), may hold values from -0.0234375 to 0.0234375
- task_cd: int32 [16384], P(('row', 'col')), may hold values from 0 to 7, as said below
- task_ab: int32 [16384], P(('row', 'col')), may hold values from 0 to 7
- task_count: int32 [256], P(('row', 'col')), may hold values from 8 to 64, as said below
Outputs:
- residual: bfloat16 [1024, 64, 256], P('col', 'row')
The draws below stay inside these ranges and needn't reach their ends.
Inputs may be any that keep to these rules, and one draw needn't show every extreme that they name: On each device the slots name distinct (task_cd, task_ab) pairs. The live slots of a device are its first task_count ones; some device has all 64 slots live in every draw.
All inputs are finite; a program needn't handle non-finite values.
Results may differ from the reference program's by a relative error of at most 0.001.
Values may be sent and summed in bfloat16 or wider, within the bound.
A program may use at most 128 MiB of HBM per device.

```python
import jax
import jax.numpy as jnp
from jax import lax

TILE_PAIRS = 256
CD_COL = 8
PAIR_TILES_ROW = 8
DEVICE_SLOTS = 64
OCC = 1024
NCD = 256
TOTAL_SLOTS = 16384
N_ROW = 8
N_COL = 32


def task_tables(key):
    base = jax.random.fold_in(key, 7131)
    groups = N_ROW * N_COL
    keys = jax.random.split(jax.random.fold_in(base, 1), groups)

    def pick(one_key):
        return jax.random.permutation(one_key, CD_COL * PAIR_TILES_ROW)[:DEVICE_SLOTS].astype(jnp.int32)
    pairs = jax.vmap(pick)(keys).reshape(groups * DEVICE_SLOTS)
    shifts = jax.random.randint(jax.random.fold_in(base, 2), (groups,), 0, 4).astype(jnp.int32)
    counts = jnp.right_shift(jnp.full((groups,), DEVICE_SLOTS, jnp.int32), shifts)
    counts = jnp.maximum(counts, max(DEVICE_SLOTS // 8, 1))
    heavy = jax.random.randint(jax.random.fold_in(base, 3), (), 0, groups).astype(jnp.int32)
    counts = jnp.where(jnp.arange(groups, dtype=jnp.int32) == heavy, DEVICE_SLOTS, counts).astype(jnp.int32)
    return (pairs // PAIR_TILES_ROW, pairs % PAIR_TILES_ROW, counts)


def draw_task_cd(key, part):
    return task_tables(key)[0]


def draw_task_ab(key, part):
    return task_tables(key)[1]


def draw_task_count(key, part):
    return task_tables(key)[2]


def levels(stream_key, dims, pieces, low, high):
    loudness, own = 1.0, jax.random.fold_in(stream_key, 6)
    for axis_at, blocks in pieces:
        heights = jnp.exp(jax.random.uniform(jax.random.fold_in(own, axis_at), (blocks,), jnp.float32, low / len(pieces), high / len(pieces)))
        loudness = loudness * jnp.repeat(heights, dims[axis_at] // blocks).reshape([-1 if axis == axis_at else 1 for axis in range(len(dims))])
    return loudness


def normal_values(key, extent, width, limit, shards=(), kind=jnp.bfloat16):
    result = width * jax.random.normal(key, extent, jnp.float32)
    if shards:
        result = result * levels(key, extent, shards, -0.22, 0.18)
    return jnp.clip(result, -limit, limit).astype(kind)


def setup_inputs(seed: int = 0) -> dict:
    key_list = jax.random.split(jax.random.key(seed), 6)
    return {
        "amps": normal_values(key_list[0], (OCC, NCD, TILE_PAIRS), 1.0, 6.0, ((0, 8), (1, 32))),
        "ints": normal_values(key_list[1], (TOTAL_SLOTS, TILE_PAIRS, TILE_PAIRS), (TILE_PAIRS * N_COL * DEVICE_SLOTS // PAIR_TILES_ROW) ** -0.5, 0.0234375, ((0, 256),)),
        "task_cd": draw_task_cd(jax.random.fold_in(key_list[5], 71), 0),
        "task_ab": draw_task_ab(jax.random.fold_in(key_list[5], 71), 0),
        "task_count": draw_task_count(jax.random.fold_in(key_list[5], 71), 0),
    }


def reference(amps, ints, task_cd, task_ab, task_count):
    occ = amps.shape[0]
    ints_dev = ints.reshape(N_ROW, N_COL, DEVICE_SLOTS, TILE_PAIRS, TILE_PAIRS)
    device_cd_tiles = task_cd.reshape(N_ROW, N_COL, DEVICE_SLOTS)
    ab_dev = task_ab.reshape(N_ROW, N_COL, DEVICE_SLOTS)
    count_dev = task_count.reshape(N_ROW, N_COL)

    def one_row(row_index):
        def one_col(total, col_index):
            def one_slot(slot, acc):
                def add_term(inner):
                    cd_tile = (col_index * CD_COL + device_cd_tiles[row_index, col_index, slot]).astype(jnp.int32)
                    tile_amps = lax.dynamic_slice_in_dim(amps, cd_tile, 1, 1)[:, 0, :]
                    term = jnp.dot(tile_amps, ints_dev[row_index, col_index, slot], preferred_element_type=jnp.float32)
                    place = ab_dev[row_index, col_index, slot].astype(jnp.int32)
                    old = lax.dynamic_slice_in_dim(inner, place, 1, 1)
                    return lax.dynamic_update_slice_in_dim(inner, old + term[:, None, :], place, 1)

                return lax.cond(slot < count_dev[row_index, col_index], add_term, lambda inner: inner, acc)

            total = lax.fori_loop(0, DEVICE_SLOTS, one_slot, total)
            return total, None

        start = jnp.zeros((occ, PAIR_TILES_ROW, TILE_PAIRS), jnp.float32)
        total, _ = lax.scan(one_col, start, jnp.arange(N_COL, dtype=jnp.int32))
        return total

    blocks = lax.map(one_row, jnp.arange(N_ROW, dtype=jnp.int32))
    whole = jnp.transpose(blocks, (1, 0, 2, 3)).reshape(occ, N_ROW * PAIR_TILES_ROW, TILE_PAIRS)
    return whole.astype(jnp.bfloat16)
```

```python
import functools

import jax
import jax.numpy as jnp
from jax import lax
from jax.experimental import pallas as pl
from jax.experimental.pallas import tpu as pltpu
from jax.sharding import PartitionSpec as P

MESH = pl.DeviceIdType.MESH
NX, NY, NZ = 4, 4, 8
TILE = 256
KT = 8
AT = 8
WIDE = AT * TILE
LANES = WIDE // 128
STEPS, GROUPS = 4, 8
TOP = 32000.0
OCTAVE = 16.0
HALF_MSG = GROUPS * LANES // 4 + 1
FULL_MSG = GROUPS * LANES // 2 + 1
ROW_MSG = LANES // 2 + 1


def place(delta, core, q):
    if delta == 0:
        return 0, core * 4 + q
    if delta == 2:
        return 2 + q // 2, 4 + core * 2 + q % 2
    d = 0 if delta == 1 else 1
    if q < 2:
        return 1, d * 4 + core * 2 + q
    return q, d * 2 + core


def group_of(step, g, y):
    if step == 0:
        return 2 * y + g // 4, g % 4
    if step == 1:
        delta, core, q = 1 + 2 * (g // 4), (g // 2) % 2, g % 2
    else:
        first = g < 4
        delta = jnp.where(first, 1 + 2 * (g // 2), 2)
        core = jnp.where(first, g % 2, (g - 4) // 2)
        q = jnp.where(first, step, 2 * (step - 2) + g % 2)
    return 2 * lax.rem(y + delta, NY) + core, q


def kernel(
    amps_ref, ints_ref, cd_ref, ab_ref, count_ref, out_ref,
    tiles, wide, table_v, table_s, lhs, part, hs, hr, fs, fr, zs, zr, own,
    ints_sem, table_sem, core_send, y_send, ag_recv,
    h_send, h_recv, f_send, f_recv, z_send, z_recv,
):
    row, col = lax.axis_index("row"), lax.axis_index("col")
    y, core = row // 2, row % 2
    z, x = col // NX, col % NX
    partner = (2 * y + 1 - core, col)
    y_up = (2 * lax.rem(y + 1, NY) + core, col)
    y_down = (2 * lax.rem(y + NY - 1, NY) + core, col)
    x_right, x_left = lax.rem(x + 1, NX), lax.rem(x + NX - 1, NX)
    right, left = (row, z * NX + x_right), (row, z * NX + x_left)
    lane = lax.broadcasted_iota(jnp.int32, (8, 128), 1)

    barrier = pltpu.get_barrier_semaphore()
    for peer in (partner, y_up, y_down, right, left):
        pl.semaphore_signal(barrier, inc=1, device_id=peer, device_id_type=MESH)
    for dz in range(1, NZ):
        peer = (row, lax.rem(z + dz, NZ) * NX + x)
        pl.semaphore_signal(barrier, inc=1, device_id=peer, device_id_type=MESH)

    load = pltpu.make_async_copy(ints_ref, tiles.at[pl.ds(0, KT * AT)], ints_sem)
    load.start()

    whole = amps_ref[...].astype(jnp.float32).reshape(128 * KT, TILE)
    for side in range(2):
        wide[side] = whole[:, side * 128 : (side + 1) * 128]
    for q in range(4):
        start = pl.multiple_of((core * 4 + q) * 32, 32)
        for k in range(KT):
            for side in range(2):
                rows = [wide[side, pl.ds((32 * xd + 8 * q) * KT + k, 8, stride=KT), :] for xd in range(NX)]
                at = k * TILE + side * 128
                lhs[0, pl.ds(start, 32), at : at + 128] = jnp.concatenate(rows, 0).astype(jnp.bfloat16)

    pl.semaphore_wait(barrier, 12)

    def block(step, g):
        return lhs.at[step, pl.ds(pl.multiple_of(g * 32, 32), 32), :]

    def send(src, dst, send_sem, recv_sem, to):
        copy = pltpu.make_async_remote_copy(
            src_ref=src, dst_ref=dst, send_sem=send_sem, recv_sem=recv_sem, device_id=to, device_id_type=MESH
        )
        copy.start()
        return copy

    def arrived(ref, sem):
        pltpu.make_async_remote_copy(
            src_ref=ref, dst_ref=ref, send_sem=core_send.at[0, 0], recv_sem=sem, device_id=partner, device_id_type=MESH
        ).wait_recv()

    pending = []
    mine = [block(0, core * 4 + q) for q in range(4)]
    for q in range(4):
        s, g = place(0, core, q)
        pending.append(send(mine[q], mine[q], core_send.at[0, q], ag_recv.at[s, g], partner))
    for q in range(4):
        s, g = place(3, core, q)
        pending.append(send(mine[q], block(s, g), y_send.at[0, q], ag_recv.at[s, g], y_up))
        s, g = place(1, core, q)
        pending.append(send(mine[q], block(s, g), y_send.at[1, q], ag_recv.at[s, g], y_down))

    def pass_on(delta, q):
        s, g = place(delta, core, q)
        arrived(block(s, g), ag_recv.at[s, g])
        pending.append(send(block(s, g), block(s, g), core_send.at[delta, q], ag_recv.at[s, g], partner))
        s2, g2 = place(2, core, q)
        if delta == 1 and q % 2 == 0:
            pending.append(send(block(s, g), block(s2, g2), y_send.at[2, q], ag_recv.at[s2, g2], y_down))
        if delta == 3 and q % 2 == 1:
            pending.append(send(block(s, g), block(s2, g2), y_send.at[2, q], ag_recv.at[s2, g2], y_up))

    def from_partner(delta, q):
        s, g = place(delta, 1 - core, q)
        arrived(block(s, g), ag_recv.at[s, g])

    count = count_ref[0]

    def note(slot, table):
        key = jnp.where(slot < count, ab_ref[slot] * KT + cd_ref[slot], -1)
        return jnp.where(lane == key, slot, table)

    table_v[...] = lax.fori_loop(0, KT * AT, note, jnp.full((8, 128), KT * AT, jnp.int32))
    tiles[KT * AT] = jnp.zeros((TILE, TILE), jnp.bfloat16)
    move = pltpu.make_async_copy(table_v, table_s, table_sem)
    move.start()
    move.wait()
    load.wait()

    def multiply(step):
        def one(a, carry):
            total = None
            for k in range(KT):
                term = jnp.dot(
                    lhs[step, :, k * TILE : (k + 1) * TILE],
                    tiles[table_s[0, a * KT + k]],
                    preferred_element_type=jnp.float32,
                )
                total = term if total is None else total + term
            part[step, :, pl.ds(pl.multiple_of(a * TILE, TILE), TILE)] = total
            return carry

        lax.fori_loop(0, AT, one, 0)

    def scale_of(code):
        return jnp.exp2(code * (1.0 / OCTAVE)) * (1.0 / TOP)

    def encode(values, store):
        top = functools.reduce(jnp.maximum, [jnp.abs(v) for v in values])
        top = jnp.maximum(jnp.max(top, axis=1, keepdims=True), 1e-30)
        code = jnp.ceil(jnp.log2(top) * OCTAVE)
        factor = 1.0 / scale_of(code)
        codes = [jnp.round(v * factor).astype(jnp.int32) for v in values]
        half = len(values) // 2
        for c in range(half):
            store(c, jnp.concatenate([codes[c], codes[c + half]], 0).astype(jnp.int16))
        return code

    def decode(words, scale):
        pairs = [w.astype(jnp.int32).astype(jnp.float32) for w in words]
        return [p[:8] * scale for p in pairs] + [p[8:] * scale for p in pairs]

    def two_rows(code):
        code = code.astype(jnp.int32)
        return jnp.concatenate([code, code], 0).astype(jnp.int16)

    def scales_in(message):
        return scale_of(message.astype(jnp.int32).astype(jnp.float32)[:8])

    def scale_at(scales, g):
        return jnp.sum(jnp.where(lane == g, scales, 0.0), axis=1, keepdims=True)

    def partial_row(step, g, xd, first, last):
        rows = pl.ds(pl.multiple_of(g * 32 + xd * 8, 8), 8)
        return [part[step, rows, c * 128 : (c + 1) * 128] for c in range(first, last)]

    half = LANES // 2

    def send_halves(step):
        across = lax.rem(x + 2, NX)
        for way, to in ((0, right), (1, left)):
            def one(g, codes, way=way):
                values = partial_row(step, g, across, way * half, (way + 1) * half)

                def store(c, word):
                    hs[step, way, g * (half // 2) + c] = word

                return jnp.where(lane == g, encode(values, store), codes)

            codes = lax.fori_loop(0, GROUPS, one, jnp.zeros((8, 128), jnp.float32))
            hs[step, way, HALF_MSG - 1] = two_rows(codes)
            pending.append(send(hs.at[step, way], hr.at[step, way], h_send.at[step, way], h_recv.at[step, way], to))

    def send_full(step):
        for way, to, xd in ((0, right, x_right), (1, left, x_left)):
            arrived(hr.at[step, way], h_recv.at[step, way])
            scales = scales_in(hr[step, way, HALF_MSG - 1])

            def one(g, codes, way=way, xd=xd, scales=scales):
                values = partial_row(step, g, xd, 0, LANES)
                words = [hr[step, way, g * (half // 2) + c] for c in range(half // 2)]
                added = decode(words, scale_at(scales, g))
                for c in range(half):
                    values[way * half + c] = values[way * half + c] + added[c]

                def store(c, word):
                    fs[step, way, g * half + c] = word

                return jnp.where(lane == g, encode(values, store), codes)

            codes = lax.fori_loop(0, GROUPS, one, jnp.zeros((8, 128), jnp.float32))
            fs[step, way, FULL_MSG - 1] = two_rows(codes)
            pending.append(send(fs.at[step, way], fr.at[step, way], f_send.at[step, way], f_recv.at[step, way], to))

    def row_copy(step, g, zd, q):
        return pltpu.make_async_remote_copy(
            src_ref=zs.at[step, g], dst_ref=zr.at[z, q], send_sem=z_send.at[step, g], recv_sem=z_recv.at[z, q],
            device_id=(row, zd * NX + x), device_id_type=MESH,
        )

    def send_rows(step):
        scales = []
        for way in range(2):
            arrived(fr.at[step, way], f_recv.at[step, way])
            scales.append(scales_in(fr[step, way, FULL_MSG - 1]))

        def one(g, carry):
            values = partial_row(step, g, x, 0, LANES)
            for way in range(2):
                words = [fr[step, way, g * half + c] for c in range(half)]
                added = decode(words, scale_at(scales[way], g))
                values = [v + w for v, w in zip(values, added)]
            zd, q = group_of(step, g, y)

            @pl.when(zd == z)
            def _():
                for c in range(LANES):
                    own[q, :, c * 128 : (c + 1) * 128] = values[c]

            @pl.when(zd != z)
            def _():
                def store(c, word):
                    zs[step, g, c] = word

                code = encode(values, store)
                zs[step, g, ROW_MSG - 1] = two_rows(jnp.broadcast_to(code, (8, 128)))
                row_copy(step, g, zd, q).start()

            return carry

        lax.fori_loop(0, GROUPS, one, 0)

    for q in range(4):
        from_partner(0, q)
    multiply(0)
    send_halves(0)

    for q in range(2):
        pass_on(1, q)
        pass_on(3, q)
    send_full(0)
    for q in range(2):
        from_partner(1, q)
        from_partner(3, q)
    multiply(1)
    send_halves(1)

    pass_on(1, 2)
    pass_on(3, 2)
    pass_on(1, 3)
    pass_on(3, 3)
    send_full(1)
    send_rows(0)
    pass_on(2, 0)
    pass_on(2, 1)
    from_partner(1, 2)
    from_partner(3, 2)
    from_partner(2, 0)
    from_partner(2, 1)
    multiply(2)
    send_halves(2)

    pass_on(2, 2)
    pass_on(2, 3)
    send_full(2)
    send_rows(1)
    from_partner(1, 3)
    from_partner(3, 3)
    from_partner(2, 2)
    from_partner(2, 3)
    multiply(3)
    send_halves(3)
    send_rows(2)
    send_full(3)
    send_rows(3)

    def gather(n, carry):
        source, q = lax.rem(z + 1 + n // 4, NZ), n % 4
        arrived(zr.at[source, q], z_recv.at[source, q])
        scale = scales_in(zr[source, q, ROW_MSG - 1])
        added = decode([zr[source, q, c] for c in range(half)], scale)
        for c in range(LANES):
            own[q, :, c * 128 : (c + 1) * 128] += added[c]
        return carry

    lax.fori_loop(0, (NZ - 1) * 4, gather, 0)
    for a in range(AT):
        for side in range(2):
            at = a * TILE + side * 128
            wide[side, pl.ds(a, 32, stride=AT), :] = own[:, :, at : at + 128].reshape(32, 128)
    for side in range(2):
        rows = wide[side, pl.ds(0, 32 * AT), :].reshape(32, AT, 128)
        out_ref[:, :, side * 128 : (side + 1) * 128] = rows.astype(jnp.bfloat16)

    for copy in pending:
        copy.wait_send()
    for step in range(STEPS):
        def drain(g, carry, step=step):
            zd, q = group_of(step, g, y)

            @pl.when(zd != z)
            def _():
                row_copy(step, g, zd, q).wait_send()

            return carry

        lax.fori_loop(0, GROUPS, drain, 0)


def shards(amps, ints, task_cd, task_ab, task_count):
    smem = pl.BlockSpec(memory_space=pltpu.SMEM)
    vmem = pl.BlockSpec(memory_space=pltpu.VMEM)
    dma = pltpu.SemaphoreType.DMA
    return pl.pallas_call(
        kernel,
        out_shape=jax.ShapeDtypeStruct((32, AT, TILE), jnp.bfloat16),
        in_specs=[vmem, pl.BlockSpec(memory_space=pl.ANY), smem, smem, smem],
        out_specs=vmem,
        scratch_shapes=[
            pltpu.VMEM((KT * AT + 1, TILE, TILE), jnp.bfloat16),
            pltpu.VMEM((2, 128 * KT, 128), jnp.float32),
            pltpu.VMEM((8, 128), jnp.int32),
            pltpu.SMEM((8, 128), jnp.int32),
            pltpu.VMEM((STEPS, 32 * GROUPS, KT * TILE), jnp.bfloat16),
            pltpu.VMEM((STEPS, 32 * GROUPS, WIDE), jnp.float32),
            pltpu.VMEM((STEPS, 2, HALF_MSG, 16, 128), jnp.int16),
            pltpu.VMEM((STEPS, 2, HALF_MSG, 16, 128), jnp.int16),
            pltpu.VMEM((STEPS, 2, FULL_MSG, 16, 128), jnp.int16),
            pltpu.VMEM((STEPS, 2, FULL_MSG, 16, 128), jnp.int16),
            pltpu.VMEM((STEPS, GROUPS, ROW_MSG, 16, 128), jnp.int16),
            pltpu.VMEM((NZ, 4, ROW_MSG, 16, 128), jnp.int16),
            pltpu.VMEM((4, 8, WIDE), jnp.float32),
            dma, dma, dma((4, 4)), dma((3, 4)), dma((STEPS, GROUPS)),
            dma((STEPS, 2)), dma((STEPS, 2)), dma((STEPS, 2)), dma((STEPS, 2)),
            dma((STEPS, GROUPS)), dma((NZ, 4)),
        ],
        compiler_params=pltpu.CompilerParams(
            collective_id=0, has_side_effects=True, vmem_limit_bytes=60 * 1024 * 1024
        ),
    )(amps, ints, task_cd, task_ab, task_count)


def solution(mesh):
    in_specs = (P("row", "col", None), P(("row", "col"), None, None)) + (P(("row", "col")),) * 3
    return jax.shard_map(
        shards, mesh=mesh, in_specs=in_specs, out_specs=P("col", "row", None), check_vma=False
    )
```

```python
import functools

import jax
import jax.numpy as jnp
from jax import lax
from jax.experimental import pallas as pl
from jax.experimental.pallas import tpu as pltpu
from jax.sharding import PartitionSpec as P

MESH = pl.DeviceIdType.MESH
NX, NY, NZ = 4, 4, 8
TILE = 256
KT = 8
AT = 8
WIDE = AT * TILE
LANES = WIDE // 128
HALF = LANES // 2
STEPS, UNITS = 4, 4
LOADS = 4
TOP = 32000.0
OCTAVE = 16.0
HALF_MSG = 2 * HALF + 1
ROW_MSG = 2 * LANES + 1


def place(delta, core, h):
    if delta == 0:
        return 0, core * 2 + h
    if delta == 2:
        return 2 + h, 2 + core
    if h == 0:
        return 1, core + (0 if delta == 1 else 2)
    return (2 if delta == 1 else 3), core


def unit_of(step, u, y):
    if step == 0:
        return 2 * y + u // 2, u % 2
    first, core = u < 2, u % 2
    if step == 1:
        delta, h = jnp.where(first, 1, 3), 0
    elif step == 2:
        delta, h = jnp.where(first, 1, 2), jnp.where(first, 1, 0)
    else:
        delta, h = jnp.where(first, 3, 2), 1
    return 2 * lax.rem(y + delta, NY) + core, h


def kernel(
    amps_ref, ints_ref, cd_ref, ab_ref, count_ref, out_ref,
    tiles, wide, table_v, table_s, lhs, part, hs, hr, fs, fr, zs, cr, zr,
    ints_sem, table_sem, block_sent, rows_sent, h_sent, f_sent, z_sent,
    ag_recv, h_recv, f_recv, c_recv, z_recv,
):
    row, col = lax.axis_index("row"), lax.axis_index("col")
    y, core = row // 2, row % 2
    z, x = col // NX, col % NX
    partner = (2 * y + 1 - core, col)
    y_up = (2 * lax.rem(y + 1, NY) + core, col)
    y_down = (2 * lax.rem(y + NY - 1, NY) + core, col)
    x_right, x_left, x_across = lax.rem(x + 1, NX), lax.rem(x + NX - 1, NX), lax.rem(x + 2, NX)
    right, left = (row, z * NX + x_right), (row, z * NX + x_left)
    lane = lax.broadcasted_iota(jnp.int32, (8, 128), 1)

    barrier = pltpu.get_barrier_semaphore()
    for peer in (partner, y_up, y_down, right, left):
        pl.semaphore_signal(barrier, inc=1, device_id=peer, device_id_type=MESH)
    for dz in (1, 2, NZ - 2, NZ - 1):
        peer = (row, lax.rem(z + dz, NZ) * NX + x)
        pl.semaphore_signal(barrier, inc=1, device_id=peer, device_id_type=MESH)

    loads = []
    for n in range(LOADS):
        some = pl.ds(n * (KT * AT // LOADS), KT * AT // LOADS)
        loads.append(pltpu.make_async_copy(ints_ref.at[some], tiles.at[some], ints_sem.at[n]))
        loads[-1].start()

    whole = amps_ref[...].astype(jnp.float32).reshape(128 * KT, TILE)
    for side in range(2):
        wide[side] = whole[:, side * 128 : (side + 1) * 128]
    for h in range(2):
        start = pl.multiple_of((core * 2 + h) * 64, 64)
        for k in range(KT):
            for side in range(2):
                rows = [wide[side, pl.ds((32 * xd + 16 * h) * KT + k, 16, stride=KT), :] for xd in range(NX)]
                at = k * TILE + side * 128
                lhs[0, pl.ds(start, 64), at : at + 128] = jnp.concatenate(rows, 0).astype(jnp.bfloat16)

    count = count_ref[0]

    def note(slot, table):
        key = jnp.where(slot < count, ab_ref[slot] * KT + cd_ref[slot], -1)
        return jnp.where(lane == key, slot, table)

    table_v[...] = lax.fori_loop(0, KT * AT, note, jnp.full((8, 128), KT * AT, jnp.int32))
    tiles[KT * AT] = jnp.zeros((TILE, TILE), jnp.bfloat16)
    move = pltpu.make_async_copy(table_v, table_s, table_sem)
    move.start()
    move.wait()
    pl.semaphore_wait(barrier, 9)

    def send(src, dst, send_sem, recv_sem, to):
        copy = pltpu.make_async_remote_copy(
            src_ref=src, dst_ref=dst, send_sem=send_sem, recv_sem=recv_sem, device_id=to, device_id_type=MESH
        )
        copy.start()

    def arrived(ref, sem):
        pltpu.make_async_remote_copy(
            src_ref=ref, dst_ref=ref, send_sem=block_sent, recv_sem=sem, device_id=partner, device_id_type=MESH
        ).wait_recv()

    def quarter(step, unit, e):
        return lhs.at[step, pl.ds(pl.multiple_of(unit * 64 + e * 32, 32), 32), :]

    def own_block(which):
        return lhs.at[0, pl.ds(pl.multiple_of(which * 128, 128), 128), :]

    def to_neighbours(h, e):
        mine = quarter(0, core * 2 + h, e)
        for delta, to in ((3, y_up), (1, y_down)):
            s, u = place(delta, core, h)
            send(mine, quarter(s, u, e), rows_sent, ag_recv.at[s, u, e], to)

    def pass_on(delta, h, e):
        s, u = place(delta, core, h)
        ref = quarter(s, u, e)
        arrived(ref, ag_recv.at[s, u, e])
        send(ref, ref, rows_sent, ag_recv.at[s, u, e], partner)
        if (delta, e) in ((1, 0), (3, 1)):
            s2, u2 = place(2, core, h)
            send(ref, quarter(s2, u2, e), rows_sent, ag_recv.at[s2, u2, e], y_down if delta == 1 else y_up)

    def from_partner(delta, h):
        s, u = place(delta, 1 - core, h)
        for e in range(2):
            arrived(quarter(s, u, e), ag_recv.at[s, u, e])

    send(own_block(core), own_block(core), block_sent, ag_recv.at[0, core, 0], partner)
    to_neighbours(0, 0)
    to_neighbours(0, 1)
    to_neighbours(1, 0)
    for copy in loads:
        copy.wait()

    def multiply(step, first=0, count=64 * UNITS, low=0, high=AT):
        rows = pl.ds(pl.multiple_of(first, 128), count)

        def one(a, carry):
            total = None
            for k in range(KT):
                term = jnp.dot(
                    lhs[step, rows, k * TILE : (k + 1) * TILE],
                    tiles[table_s[0, a * KT + k]],
                    preferred_element_type=jnp.float32,
                )
                total = term if total is None else total + term
            part[step, rows, pl.ds(pl.multiple_of(a * TILE, TILE), TILE)] = total
            return carry

        lax.fori_loop(low, high, one, 0)

    def encode(values, message):
        top = functools.reduce(jnp.maximum, [jnp.abs(v) for v in values])
        top = jnp.maximum(jnp.max(top, axis=1, keepdims=True), 1e-30)
        code = jnp.ceil(jnp.log2(top) * OCTAVE)
        factor = jnp.exp2(code * (-1.0 / OCTAVE)) * TOP
        for c, v in enumerate(values):
            message[c] = jnp.round(v * factor).astype(jnp.int32).astype(jnp.int16)
        message[len(values)] = jnp.broadcast_to(code, (8, 128)).astype(jnp.int32).astype(jnp.int16)

    def decode(message, n):
        def wide_of(c):
            return message[c].astype(jnp.int32).astype(jnp.float32)

        scale = jnp.exp2(wide_of(n) * (1.0 / OCTAVE)) * (1.0 / TOP)
        return [wide_of(c) * scale for c in range(n)]

    def rows_of(u, xd, i):
        return pl.ds(pl.multiple_of(u * 64 + xd * 16 + i * 8, 8), 8)

    def values_of(step, u, xd, first, last):
        return [part[step, rows_of(u, xd, i), c * 128 : (c + 1) * 128] for i in range(2) for c in range(first, last)]

    def add_into(step, u, xd, added):
        total = [v + w for v, w in zip(values_of(step, u, xd, 0, LANES), added)]
        for n, v in enumerate(total):
            part[step, rows_of(u, xd, n // LANES), n % LANES * 128 : (n % LANES + 1) * 128] = v
        return total

    def half_copy(step, u, way):
        return pltpu.make_async_remote_copy(
            src_ref=hs.at[step, u, way], dst_ref=hr.at[step, u, way], send_sem=h_sent,
            recv_sem=h_recv.at[step, u, way], device_id=(right, left)[way], device_id_type=MESH,
        )

    def full_copy(step, u, way):
        return pltpu.make_async_remote_copy(
            src_ref=fs.at[step, u, way], dst_ref=fr.at[step, u, way], send_sem=f_sent,
            recv_sem=f_recv.at[step, u, way], device_id=(right, left)[way], device_id_type=MESH,
        )

    def offset(zd):
        return lax.rem(z - zd + NZ + NZ // 2, NZ) - NZ // 2

    def row_copy(step, u, zd, h):
        off = offset(zd)
        slot = jnp.where(off < 0, off + 2, off + 1)
        return pltpu.make_async_remote_copy(
            src_ref=zs.at[step * UNITS + u], dst_ref=zr.at[slot, h], send_sem=z_sent, recv_sem=z_recv.at[slot, h],
            device_id=(row, zd * NX + x), device_id_type=MESH,
        )

    def collect_copy(step, u, off):
        ahead = jnp.where(off == -4, 2, jnp.where(off == -3, 1, NZ - 1))
        slot = jnp.where(off == -4, 1, 0)
        return pltpu.make_async_remote_copy(
            src_ref=zs.at[step * UNITS + u], dst_ref=cr.at[step, u, slot], send_sem=z_sent,
            recv_sem=c_recv.at[step, u, slot], device_id=(row, lax.rem(z + ahead, NZ) * NX + x), device_id_type=MESH,
        )

    def stage_half(step, way, first=0, count=UNITS):
        def body(n, carry):
            u = first + n
            encode(values_of(step, u, x_across, way * HALF, (way + 1) * HALF), hs.at[step, u, way])
            half_copy(step, u, way).start()
            return carry

        lax.fori_loop(0, count, body, 0)

    def stage_full(step, way, first=0):
        def body(n, carry):
            u = lax.rem(first + n, UNITS)
            arrived(hr.at[step, u, way], h_recv.at[step, u, way])
            values = values_of(step, u, x_right if way == 0 else x_left, 0, LANES)
            for n, v in enumerate(decode(hr.at[step, u, way], 2 * HALF)):
                at = n // HALF * LANES + way * HALF + n % HALF
                values[at] = values[at] + v
            encode(values, fs.at[step, u, way])
            full_copy(step, u, way).start()
            return carry

        lax.fori_loop(0, UNITS, body, 0)

    def stage_rows(step, first=0):
        def body(n, carry):
            u = lax.rem(first + n, UNITS)
            zd, h = unit_of(step, u, y)
            off = offset(zd)
            for way in range(2):
                arrived(fr.at[step, u, way], f_recv.at[step, u, way])
            added = [v + w for v, w in zip(*[decode(fr.at[step, u, way], 2 * LANES) for way in range(2)])]
            encode(add_into(step, u, x, added), zs.at[step * UNITS + u])

            @pl.when((off == 1) | (off == -1))
            def _():
                row_copy(step, u, zd, h).start()

            @pl.when((off == 3) | (off < -2))
            def _():
                collect_copy(step, u, off).start()

            return carry

        lax.fori_loop(0, UNITS, body, 0)

    def stage_collect(step, first=0):
        def body(n, carry):
            u = lax.rem(first + n, UNITS)
            zd, h = unit_of(step, u, y)
            off = offset(zd)

            def take(slot):
                arrived(cr.at[step, u, slot], c_recv.at[step, u, slot])
                return decode(cr.at[step, u, slot], 2 * LANES)

            @pl.when(off == -2)
            def _():
                add_into(step, u, x, take(1))

            @pl.when((off == 2) | (off == -2))
            def _():
                encode(add_into(step, u, x, take(0)), zs.at[step * UNITS + u])
                row_copy(step, u, zd, h).start()

            return carry

        lax.fori_loop(0, UNITS, body, 0)

    multiply(0, core * 128, 128, 0, 4)
    stage_half(0, 0, core * 2, 2)
    multiply(0, core * 128, 128, 4, 8)
    stage_half(0, 1, core * 2, 2)
    arrived(own_block(1 - core), ag_recv.at[0, 1 - core, 0])
    multiply(0, 128 - core * 128, 128, 0, 4)
    stage_half(0, 0, 2 - core * 2, 2)
    multiply(0, 128 - core * 128, 128, 4, 8)
    stage_half(0, 1, 2 - core * 2, 2)
    pass_on(1, 0, 0)
    pass_on(3, 0, 0)
    pass_on(1, 0, 1)
    pass_on(3, 0, 1)
    to_neighbours(1, 1)
    stage_full(0, 0, core * 2)
    stage_full(0, 1, core * 2)

    pass_on(1, 1, 0)
    pass_on(3, 1, 0)
    from_partner(1, 0)
    from_partner(3, 0)
    multiply(1, low=0, high=4)
    stage_half(1, 0)
    multiply(1, low=4, high=8)
    stage_half(1, 1)
    pass_on(2, 0, 0)
    pass_on(2, 0, 1)
    stage_rows(0, core * 2)
    pass_on(1, 1, 1)
    pass_on(3, 1, 1)
    stage_full(1, 0)
    stage_full(1, 1)

    from_partner(1, 1)
    from_partner(2, 0)
    multiply(2, low=0, high=4)
    stage_half(2, 0)
    pass_on(2, 1, 0)
    pass_on(2, 1, 1)
    multiply(2, low=4, high=8)
    stage_half(2, 1)
    stage_collect(0, core * 2)

    from_partner(3, 1)
    from_partner(2, 1)
    multiply(3, low=0, high=4)
    stage_half(3, 0)
    stage_full(2, 0)
    multiply(3, low=4, high=8)
    stage_half(3, 1)
    stage_full(2, 1)
    stage_rows(1)
    stage_full(3, 0)
    stage_full(3, 1)
    stage_collect(1)
    stage_rows(2)
    stage_rows(3)
    stage_collect(2)
    stage_collect(3)

    up, mine_core = lax.rem(z // 2 - y + NY, NY), z % 2
    for h in range(2):
        places = [place(delta, mine_core, h) for delta in range(NY)]
        step, u = places[0]
        for delta in range(1, NY):
            step = jnp.where(up == delta, places[delta][0], step)
            u = jnp.where(up == delta, places[delta][1], u)
        total = values_of(step, u, x, 0, LANES)
        for source in range(4):
            arrived(zr.at[source, h], z_recv.at[source, h])
            total = [v + w for v, w in zip(total, decode(zr.at[source, h], 2 * LANES))]
        for n, v in enumerate(total):
            i, c = n // LANES, n % LANES
            wide[c % 2, pl.ds((h * 16 + i * 8) * AT + c // 2, 8, stride=AT), :] = v
    for side in range(2):
        rows = wide[side, pl.ds(0, 32 * AT), :].reshape(32, AT, 128)
        out_ref[:, :, side * 128 : (side + 1) * 128] = rows.astype(jnp.bfloat16)

    def all_sent(ref, sem):
        pltpu.make_async_remote_copy(
            src_ref=ref, dst_ref=ref, send_sem=sem, recv_sem=z_recv.at[0, 0], device_id=partner, device_id_type=MESH
        ).wait_send()

    all_sent(own_block(core), block_sent)
    all_sent(lhs.at[pl.ds(0, 3)], rows_sent)
    all_sent(hs, h_sent)
    all_sent(fs, f_sent)
    all_sent(zs.at[pl.ds(0, STEPS * UNITS - 2)], z_sent)


def shards(amps, ints, task_cd, task_ab, task_count):
    smem = pl.BlockSpec(memory_space=pltpu.SMEM)
    vmem = pl.BlockSpec(memory_space=pltpu.VMEM)
    dma = pltpu.SemaphoreType.DMA

    def message(*shape):
        return pltpu.VMEM((*shape, 8, 128), jnp.int16)

    return pl.pallas_call(
        kernel,
        out_shape=jax.ShapeDtypeStruct((32, AT, TILE), jnp.bfloat16),
        in_specs=[vmem, pl.BlockSpec(memory_space=pl.ANY), smem, smem, smem],
        out_specs=vmem,
        scratch_shapes=[
            pltpu.VMEM((KT * AT + 1, TILE, TILE), jnp.bfloat16),
            pltpu.VMEM((2, 128 * KT, 128), jnp.float32),
            pltpu.VMEM((8, 128), jnp.int32),
            pltpu.SMEM((8, 128), jnp.int32),
            pltpu.VMEM((STEPS, 64 * UNITS, KT * TILE), jnp.bfloat16),
            pltpu.VMEM((STEPS, 64 * UNITS, WIDE), jnp.float32),
            message(STEPS, UNITS, 2, HALF_MSG), message(STEPS, UNITS, 2, HALF_MSG),
            message(STEPS, UNITS, 2, ROW_MSG), message(STEPS, UNITS, 2, ROW_MSG),
            message(STEPS * UNITS, ROW_MSG), message(STEPS, UNITS, 2, ROW_MSG), message(4, 2, ROW_MSG),
            dma((LOADS,)), dma, dma, dma, dma, dma, dma,
            dma((STEPS, UNITS, 2)), dma((STEPS, UNITS, 2)), dma((STEPS, UNITS, 2)), dma((STEPS, UNITS, 2)), dma((4, 2)),
        ],
        compiler_params=pltpu.CompilerParams(
            collective_id=0, has_side_effects=True, vmem_limit_bytes=60 * 1024 * 1024
        ),
    )(amps, ints, task_cd, task_ab, task_count)


def solution(mesh):
    in_specs = (P("row", "col", None), P(("row", "col"), None, None)) + (P(("row", "col")),) * 3
    return jax.shard_map(
        shards, mesh=mesh, in_specs=in_specs, out_specs=P("col", "row", None), check_vma=False
    )
```

```python
import functools

import jax
import jax.numpy as jnp
from jax import lax
from jax.experimental import pallas as pl
from jax.experimental.pallas import tpu as pltpu
from jax.sharding import PartitionSpec as P

MESH = pl.DeviceIdType.MESH
NX, NY, NZ = 4, 4, 8
TILE = 256
KT = 8
AT = 8
WIDE = AT * TILE
LANES = WIDE // 128
HALF = LANES // 2
STEPS, UNITS = 4, 4
LOADS = 4
TOP = 32000.0
OCTAVE = 16.0
HALF_MSG = 2 * HALF + 1
ROW_MSG = 2 * LANES + 1


def place(delta, core, h):
    if delta == 0:
        return 0, core * 2 + h
    if delta == 2:
        return 2 + h, 2 + core
    if h == 0:
        return 1, core + (0 if delta == 1 else 2)
    return (2 if delta == 1 else 3), core


def unit_of(step, u, y):
    if step == 0:
        return 2 * y + u // 2, u % 2
    first, core = u < 2, u % 2
    if step == 1:
        delta, h = jnp.where(first, 1, 3), 0
    elif step == 2:
        delta, h = jnp.where(first, 1, 2), jnp.where(first, 1, 0)
    else:
        delta, h = jnp.where(first, 3, 2), 1
    return 2 * lax.rem(y + delta, NY) + core, h


def kernel(
    amps_hbm, ints_ref, cd_ref, ab_ref, count_ref, out_ref,
    tiles, amps_ref, wide, table_v, table_s, lhs, part, hs, hr, fs, fr, zs, cr, zr,
    amps_sem, ints_sem, table_sem, block_sent, rows_sent, h_sent, f_sent, z_sent,
    ag_recv, h_recv, f_recv, c_recv, z_recv,
):
    row, col = lax.axis_index("row"), lax.axis_index("col")
    y, core = row // 2, row % 2
    z, x = col // NX, col % NX
    partner = (2 * y + 1 - core, col)
    y_up = (2 * lax.rem(y + 1, NY) + core, col)
    y_down = (2 * lax.rem(y + NY - 1, NY) + core, col)
    x_right, x_left, x_across = lax.rem(x + 1, NX), lax.rem(x + NX - 1, NX), lax.rem(x + 2, NX)
    right, left = (row, z * NX + x_right), (row, z * NX + x_left)
    lane = lax.broadcasted_iota(jnp.int32, (8, 128), 1)

    bring = pltpu.make_async_copy(amps_hbm, amps_ref, amps_sem)
    bring.start()
    barrier = pltpu.get_barrier_semaphore()
    for peer in (partner, y_up, y_down, right, left):
        pl.semaphore_signal(barrier, inc=1, device_id=peer, device_id_type=MESH)
    for dz in (1, 2, NZ - 2, NZ - 1):
        peer = (row, lax.rem(z + dz, NZ) * NX + x)
        pl.semaphore_signal(barrier, inc=1, device_id=peer, device_id_type=MESH)

    loads = []
    for n in range(LOADS):
        some = pl.ds(n * (KT * AT // LOADS), KT * AT // LOADS)
        loads.append(pltpu.make_async_copy(ints_ref.at[some], tiles.at[some], ints_sem.at[n]))
        loads[-1].start()

    bring.wait()
    whole = amps_ref[...].astype(jnp.float32).reshape(128 * KT, TILE)
    for side in range(2):
        wide[side] = whole[:, side * 128 : (side + 1) * 128]
    for h in range(2):
        start = pl.multiple_of((core * 2 + h) * 64, 64)
        for k in range(KT):
            for side in range(2):
                rows = [wide[side, pl.ds((32 * xd + 16 * h) * KT + k, 16, stride=KT), :] for xd in range(NX)]
                at = k * TILE + side * 128
                lhs[0, pl.ds(start, 64), at : at + 128] = jnp.concatenate(rows, 0).astype(jnp.bfloat16)

    count = count_ref[0]

    def note(slot, table):
        key = jnp.where(slot < count, ab_ref[slot] * KT + cd_ref[slot], -1)
        return jnp.where(lane == key, slot, table)

    table_v[...] = lax.fori_loop(0, KT * AT, note, jnp.full((8, 128), KT * AT, jnp.int32))
    tiles[KT * AT] = jnp.zeros((TILE, TILE), jnp.bfloat16)
    move = pltpu.make_async_copy(table_v, table_s, table_sem)
    move.start()
    move.wait()
    pl.semaphore_wait(barrier, 9)

    def send(src, dst, send_sem, recv_sem, to):
        copy = pltpu.make_async_remote_copy(
            src_ref=src, dst_ref=dst, send_sem=send_sem, recv_sem=recv_sem, device_id=to, device_id_type=MESH
        )
        copy.start()

    def arrived(ref, sem):
        pltpu.make_async_remote_copy(
            src_ref=ref, dst_ref=ref, send_sem=block_sent, recv_sem=sem, device_id=partner, device_id_type=MESH
        ).wait_recv()

    def quarter(step, unit, e):
        return lhs.at[step, pl.ds(pl.multiple_of(unit * 64 + e * 32, 32), 32), :]

    def own_block(which):
        return lhs.at[0, pl.ds(pl.multiple_of(which * 128, 128), 128), :]

    def to_neighbours(h, e):
        mine = quarter(0, core * 2 + h, e)
        for delta, to in ((3, y_up), (1, y_down)):
            s, u = place(delta, core, h)
            send(mine, quarter(s, u, e), rows_sent, ag_recv.at[s, u, e], to)

    def pass_on(delta, h, e):
        s, u = place(delta, core, h)
        ref = quarter(s, u, e)
        arrived(ref, ag_recv.at[s, u, e])
        send(ref, ref, rows_sent, ag_recv.at[s, u, e], partner)
        if (delta, e) in ((1, 0), (3, 1)):
            s2, u2 = place(2, core, h)
            send(ref, quarter(s2, u2, e), rows_sent, ag_recv.at[s2, u2, e], y_down if delta == 1 else y_up)

    def from_partner(delta, h):
        s, u = place(delta, 1 - core, h)
        for e in range(2):
            arrived(quarter(s, u, e), ag_recv.at[s, u, e])

    send(own_block(core), own_block(core), block_sent, ag_recv.at[0, core, 0], partner)
    to_neighbours(0, 0)
    to_neighbours(0, 1)
    to_neighbours(1, 0)
    for copy in loads:
        copy.wait()

    def multiply(step, first=0, count=64 * UNITS, low=0, high=AT):
        rows = pl.ds(pl.multiple_of(first, 128), count)

        def one(a, carry):
            total = None
            for k in range(KT):
                term = jnp.dot(
                    lhs[step, rows, k * TILE : (k + 1) * TILE],
                    tiles[table_s[0, a * KT + k]],
                    preferred_element_type=jnp.float32,
                )
                total = term if total is None else total + term
            part[step, rows, pl.ds(pl.multiple_of(a * TILE, TILE), TILE)] = total
            return carry

        lax.fori_loop(low, high, one, 0)

    def encode(values, message):
        top = functools.reduce(jnp.maximum, [jnp.abs(v) for v in values])
        top = jnp.maximum(jnp.max(top, axis=1, keepdims=True), 1e-30)
        code = jnp.ceil(jnp.log2(top) * OCTAVE)
        factor = jnp.exp2(code * (-1.0 / OCTAVE)) * TOP
        for c, v in enumerate(values):
            message[c] = jnp.round(v * factor).astype(jnp.int32).astype(jnp.int16)
        message[len(values)] = jnp.broadcast_to(code, (8, 128)).astype(jnp.int32).astype(jnp.int16)

    def decode(message, n):
        def wide_of(c):
            return message[c].astype(jnp.int32).astype(jnp.float32)

        scale = jnp.exp2(wide_of(n) * (1.0 / OCTAVE)) * (1.0 / TOP)
        return [wide_of(c) * scale for c in range(n)]

    def rows_of(u, xd, i):
        return pl.ds(pl.multiple_of(u * 64 + xd * 16 + i * 8, 8), 8)

    def values_of(step, u, xd, first, last):
        return [part[step, rows_of(u, xd, i), c * 128 : (c + 1) * 128] for i in range(2) for c in range(first, last)]

    def add_into(step, u, xd, added):
        total = [v + w for v, w in zip(values_of(step, u, xd, 0, LANES), added)]
        for n, v in enumerate(total):
            part[step, rows_of(u, xd, n // LANES), n % LANES * 128 : (n % LANES + 1) * 128] = v
        return total

    def half_copy(step, u, way):
        return pltpu.make_async_remote_copy(
            src_ref=hs.at[step, u, way], dst_ref=hr.at[step, u, way], send_sem=h_sent,
            recv_sem=h_recv.at[step, u, way], device_id=(right, left)[way], device_id_type=MESH,
        )

    def full_copy(step, u, way):
        return pltpu.make_async_remote_copy(
            src_ref=fs.at[step, u, way], dst_ref=fr.at[step, u, way], send_sem=f_sent,
            recv_sem=f_recv.at[step, u, way], device_id=(right, left)[way], device_id_type=MESH,
        )

    def offset(zd):
        return lax.rem(z - zd + NZ + NZ // 2, NZ) - NZ // 2

    def row_copy(step, u, zd, h):
        off = offset(zd)
        slot = jnp.where(off < 0, off + 2, off + 1)
        return pltpu.make_async_remote_copy(
            src_ref=zs.at[step * UNITS + u], dst_ref=zr.at[slot, h], send_sem=z_sent, recv_sem=z_recv.at[slot, h],
            device_id=(row, zd * NX + x), device_id_type=MESH,
        )

    def collect_copy(step, u, off):
        ahead = jnp.where(off == -4, jnp.where(u % 2 == 0, 2, NZ - 2), jnp.where(off == -3, 1, NZ - 1))
        slot = jnp.where(off == -4, 1, 0)
        return pltpu.make_async_remote_copy(
            src_ref=zs.at[step * UNITS + u], dst_ref=cr.at[step, u, slot], send_sem=z_sent,
            recv_sem=c_recv.at[step, u, slot], device_id=(row, lax.rem(z + ahead, NZ) * NX + x), device_id_type=MESH,
        )

    def stage_half(step, way, first=0, count=UNITS):
        def body(n, carry):
            u = first + n
            encode(values_of(step, u, x_across, way * HALF, (way + 1) * HALF), hs.at[step, u, way])
            half_copy(step, u, way).start()
            return carry

        lax.fori_loop(0, count, body, 0)

    def stage_full(step, way, first=0):
        def body(n, carry):
            u = lax.rem(first + n, UNITS)
            arrived(hr.at[step, u, way], h_recv.at[step, u, way])
            values = values_of(step, u, x_right if way == 0 else x_left, 0, LANES)
            for n, v in enumerate(decode(hr.at[step, u, way], 2 * HALF)):
                at = n // HALF * LANES + way * HALF + n % HALF
                values[at] = values[at] + v
            encode(values, fs.at[step, u, way])
            full_copy(step, u, way).start()
            return carry

        lax.fori_loop(0, UNITS, body, 0)

    def stage_rows(step, first=0, count=UNITS):
        def body(n, carry):
            u = lax.rem(first + n, UNITS)
            zd, h = unit_of(step, u, y)
            off = offset(zd)
            for way in range(2):
                arrived(fr.at[step, u, way], f_recv.at[step, u, way])
            added = [v + w for v, w in zip(*[decode(fr.at[step, u, way], 2 * LANES) for way in range(2)])]
            encode(add_into(step, u, x, added), zs.at[step * UNITS + u])

            @pl.when((off == 1) | (off == -1))
            def _():
                row_copy(step, u, zd, h).start()

            @pl.when((off == 3) | (off < -2))
            def _():
                collect_copy(step, u, off).start()

            return carry

        lax.fori_loop(0, count, body, 0)

    def stage_collect(step, first=0):
        def body(n, carry):
            u = lax.rem(first + n, UNITS)
            zd, h = unit_of(step, u, y)
            off = offset(zd)

            def take(slot):
                arrived(cr.at[step, u, slot], c_recv.at[step, u, slot])
                return decode(cr.at[step, u, slot], 2 * LANES)

            @pl.when(jnp.where(u % 2 == 0, off == -2, off == 2))
            def _():
                add_into(step, u, x, take(1))

            @pl.when((off == 2) | (off == -2))
            def _():
                encode(add_into(step, u, x, take(0)), zs.at[step * UNITS + u])
                row_copy(step, u, zd, h).start()

            return carry

        lax.fori_loop(0, UNITS, body, 0)

    multiply(0, core * 128, 128, 0, 4)
    stage_half(0, 0, core * 2, 2)
    multiply(0, core * 128, 128, 4, 8)
    stage_half(0, 1, core * 2, 2)
    arrived(own_block(1 - core), ag_recv.at[0, 1 - core, 0])
    multiply(0, 128 - core * 128, 128, 0, 4)
    stage_half(0, 0, 2 - core * 2, 2)
    multiply(0, 128 - core * 128, 128, 4, 8)
    stage_half(0, 1, 2 - core * 2, 2)
    pass_on(1, 0, 0)
    pass_on(3, 0, 0)
    pass_on(1, 0, 1)
    pass_on(3, 0, 1)
    to_neighbours(1, 1)
    stage_full(0, 0, core * 2)
    stage_full(0, 1, core * 2)

    pass_on(1, 1, 0)
    pass_on(3, 1, 0)
    from_partner(1, 0)
    from_partner(3, 0)
    multiply(1, low=0, high=4)
    stage_half(1, 0)
    multiply(1, low=4, high=8)
    stage_half(1, 1)
    pass_on(2, 0, 0)
    pass_on(2, 0, 1)
    stage_rows(0, core * 2)
    pass_on(1, 1, 1)
    pass_on(3, 1, 1)
    stage_full(1, 0)
    stage_full(1, 1)

    from_partner(1, 1)
    from_partner(2, 0)
    multiply(2, low=0, high=4)
    stage_half(2, 0)
    pass_on(2, 1, 0)
    pass_on(2, 1, 1)
    multiply(2, low=4, high=8)
    stage_half(2, 1)
    stage_collect(0, core * 2)

    from_partner(3, 1)
    from_partner(2, 1)
    multiply(3, low=4, high=8)
    stage_half(3, 1)
    stage_full(2, 0)
    stage_full(2, 1)
    stage_rows(1)
    multiply(3, low=0, high=4)
    stage_half(3, 0)
    stage_full(3, 1)
    stage_collect(1)
    stage_full(3, 0)
    stage_rows(2)
    stage_rows(3)
    stage_collect(2)
    stage_collect(3)

    up, mine_core = lax.rem(z // 2 - y + NY, NY), z % 2
    for h in range(2):
        places = [place(delta, mine_core, h) for delta in range(NY)]
        step, u = places[0]
        for delta in range(1, NY):
            step = jnp.where(up == delta, places[delta][0], step)
            u = jnp.where(up == delta, places[delta][1], u)
        total = values_of(step, u, x, 0, LANES)
        for source in range(4):
            arrived(zr.at[source, h], z_recv.at[source, h])
            total = [v + w for v, w in zip(total, decode(zr.at[source, h], 2 * LANES))]
        for n, v in enumerate(total):
            i, c = n // LANES, n % LANES
            wide[c % 2, pl.ds((h * 16 + i * 8) * AT + c // 2, 8, stride=AT), :] = v
    for side in range(2):
        rows = wide[side, pl.ds(0, 32 * AT), :].reshape(32, AT, 128)
        out_ref[:, :, side * 128 : (side + 1) * 128] = rows.astype(jnp.bfloat16)

    def all_sent(ref, sem):
        pltpu.make_async_remote_copy(
            src_ref=ref, dst_ref=ref, send_sem=sem, recv_sem=z_recv.at[0, 0], device_id=partner, device_id_type=MESH
        ).wait_send()

    all_sent(own_block(core), block_sent)
    all_sent(lhs.at[pl.ds(0, 3)], rows_sent)
    all_sent(hs, h_sent)
    all_sent(fs, f_sent)
    all_sent(zs.at[pl.ds(0, STEPS * UNITS - 2)], z_sent)


def shards(amps, ints, task_cd, task_ab, task_count):
    smem = pl.BlockSpec(memory_space=pltpu.SMEM)
    vmem = pl.BlockSpec(memory_space=pltpu.VMEM)
    dma = pltpu.SemaphoreType.DMA

    def message(*shape):
        return pltpu.VMEM((*shape, 8, 128), jnp.int16)

    return pl.pallas_call(
        kernel,
        out_shape=jax.ShapeDtypeStruct((32, AT, TILE), jnp.bfloat16),
        in_specs=[pl.BlockSpec(memory_space=pl.ANY), pl.BlockSpec(memory_space=pl.ANY), smem, smem, smem],
        out_specs=vmem,
        scratch_shapes=[
            pltpu.VMEM((KT * AT + 1, TILE, TILE), jnp.bfloat16),
            pltpu.VMEM((128, KT, TILE), jnp.bfloat16),
            pltpu.VMEM((2, 128 * KT, 128), jnp.float32),
            pltpu.VMEM((8, 128), jnp.int32),
            pltpu.SMEM((8, 128), jnp.int32),
            pltpu.VMEM((STEPS, 64 * UNITS, KT * TILE), jnp.bfloat16),
            pltpu.VMEM((STEPS, 64 * UNITS, WIDE), jnp.float32),
            message(STEPS, UNITS, 2, HALF_MSG), message(STEPS, UNITS, 2, HALF_MSG),
            message(STEPS, UNITS, 2, ROW_MSG), message(STEPS, UNITS, 2, ROW_MSG),
            message(STEPS * UNITS, ROW_MSG), message(STEPS, UNITS, 2, ROW_MSG), message(4, 2, ROW_MSG),
            dma, dma((LOADS,)), dma, dma, dma, dma, dma, dma,
            dma((STEPS, UNITS, 2)), dma((STEPS, UNITS, 2)), dma((STEPS, UNITS, 2)), dma((STEPS, UNITS, 2)), dma((4, 2)),
        ],
        compiler_params=pltpu.CompilerParams(
            collective_id=0, has_side_effects=True, vmem_limit_bytes=60 * 1024 * 1024
        ),
    )(amps, ints, task_cd, task_ab, task_count)


def solution(mesh):
    in_specs = (P("row", "col", None), P(("row", "col"), None, None)) + (P(("row", "col")),) * 3
    return jax.shard_map(
        shards, mesh=mesh, in_specs=in_specs, out_specs=P("col", "row", None), check_vma=False
    )
```

```python
import functools

import jax
import jax.numpy as jnp
from jax import lax
from jax.experimental import pallas as pl
from jax.experimental.pallas import tpu as pltpu
from jax.sharding import PartitionSpec as P

MESH = pl.DeviceIdType.MESH
NX, NY, NZ = 4, 4, 8
TILE = 256
KT = 8
AT = 8
WIDE = AT * TILE
LANES = WIDE // 128
HALF = LANES // 2
STEPS, UNITS = 4, 4
LOADS = 4
TOP = 32000.0
OCTAVE = 16.0
HALF_MSG = 2 * HALF + 1
ROW_MSG = 2 * LANES + 1


def place(delta, core, h):
    if delta == 0:
        return 0, core * 2 + h
    if delta == 2:
        return 2 + h, 2 + core
    if h == 0:
        return 1, core + (0 if delta == 1 else 2)
    return (2 if delta == 1 else 3), core


def unit_of(step, u, y):
    if step == 0:
        return 2 * y + u // 2, u % 2
    first, core = u < 2, u % 2
    if step == 1:
        delta, h = jnp.where(first, 1, 3), 0
    elif step == 2:
        delta, h = jnp.where(first, 1, 2), jnp.where(first, 1, 0)
    else:
        delta, h = jnp.where(first, 3, 2), 1
    return 2 * lax.rem(y + delta, NY) + core, h


def kernel(
    amps_hbm, ints_ref, cd_ref, ab_ref, count_ref, out_ref,
    tiles, amps_ref, wide, table_v, table_s, lhs, part, hs, hr, fs, fr, zs, cr, zr,
    amps_sem, ints_sem, table_sem, block_sent, rows_sent, h_sent, f_sent, z_sent,
    ag_recv, h_recv, f_recv, c_recv, z_recv,
):
    row, col = lax.axis_index("row"), lax.axis_index("col")
    y, core = row // 2, row % 2
    z, x = col // NX, col % NX
    partner = (2 * y + 1 - core, col)
    y_up = (2 * lax.rem(y + 1, NY) + core, col)
    y_down = (2 * lax.rem(y + NY - 1, NY) + core, col)
    x_right, x_left, x_across = lax.rem(x + 1, NX), lax.rem(x + NX - 1, NX), lax.rem(x + 2, NX)
    right, left = (row, z * NX + x_right), (row, z * NX + x_left)
    lane = lax.broadcasted_iota(jnp.int32, (8, 128), 1)

    bring = pltpu.make_async_copy(amps_hbm, amps_ref, amps_sem)
    bring.start()
    barrier = pltpu.get_barrier_semaphore()
    for peer in (partner, y_up, y_down, right, left):
        pl.semaphore_signal(barrier, inc=1, device_id=peer, device_id_type=MESH)
    for dz in (1, 2, NZ - 2, NZ - 1):
        peer = (row, lax.rem(z + dz, NZ) * NX + x)
        pl.semaphore_signal(barrier, inc=1, device_id=peer, device_id_type=MESH)

    loads = []
    for n in range(LOADS):
        some = pl.ds(n * (KT * AT // LOADS), KT * AT // LOADS)
        loads.append(pltpu.make_async_copy(ints_ref.at[some], tiles.at[some], ints_sem.at[n]))
        loads[-1].start()

    bring.wait()
    whole = amps_ref[...].astype(jnp.float32).reshape(128 * KT, TILE)
    for side in range(2):
        wide[side] = whole[:, side * 128 : (side + 1) * 128]
    for h in range(2):
        start = pl.multiple_of((core * 2 + h) * 64, 64)
        for k in range(KT):
            for side in range(2):
                rows = [wide[side, pl.ds((32 * xd + 16 * h) * KT + k, 16, stride=KT), :] for xd in range(NX)]
                at = k * TILE + side * 128
                lhs[0, pl.ds(start, 64), at : at + 128] = jnp.concatenate(rows, 0).astype(jnp.bfloat16)

    pl.semaphore_wait(barrier, 9)

    def send(src, dst, send_sem, recv_sem, to):
        copy = pltpu.make_async_remote_copy(
            src_ref=src, dst_ref=dst, send_sem=send_sem, recv_sem=recv_sem, device_id=to, device_id_type=MESH
        )
        copy.start()

    def arrived(ref, sem):
        pltpu.make_async_remote_copy(
            src_ref=ref, dst_ref=ref, send_sem=block_sent, recv_sem=sem, device_id=partner, device_id_type=MESH
        ).wait_recv()

    def quarter(step, unit, e):
        return lhs.at[step, pl.ds(pl.multiple_of(unit * 64 + e * 32, 32), 32), :]

    def own_block(which):
        return lhs.at[0, pl.ds(pl.multiple_of(which * 128, 128), 128), :]

    def to_neighbours(h, e):
        mine = quarter(0, core * 2 + h, e)
        for delta, to in ((3, y_up), (1, y_down)):
            s, u = place(delta, core, h)
            send(mine, quarter(s, u, e), rows_sent, ag_recv.at[s, u, e], to)

    def pass_on(delta, h, e):
        s, u = place(delta, core, h)
        ref = quarter(s, u, e)
        arrived(ref, ag_recv.at[s, u, e])
        send(ref, ref, rows_sent, ag_recv.at[s, u, e], partner)
        if (delta, e) in ((1, 0), (3, 1)):
            s2, u2 = place(2, core, h)
            send(ref, quarter(s2, u2, e), rows_sent, ag_recv.at[s2, u2, e], y_down if delta == 1 else y_up)

    def from_partner(delta, h):
        s, u = place(delta, 1 - core, h)
        for e in range(2):
            arrived(quarter(s, u, e), ag_recv.at[s, u, e])

    send(own_block(core), own_block(core), block_sent, ag_recv.at[0, core, 0], partner)
    to_neighbours(0, 0)
    to_neighbours(0, 1)
    to_neighbours(1, 0)
    count = count_ref[0]

    def note(slot, table):
        key = jnp.where(slot < count, ab_ref[slot] * KT + cd_ref[slot], -1)
        return jnp.where(lane == key, slot, table)

    table_v[...] = lax.fori_loop(0, KT * AT, note, jnp.full((8, 128), KT * AT, jnp.int32))
    tiles[KT * AT] = jnp.zeros((TILE, TILE), jnp.bfloat16)
    move = pltpu.make_async_copy(table_v, table_s, table_sem)
    move.start()
    move.wait()
    for copy in loads:
        copy.wait()

    def multiply(step, first=0, count=64 * UNITS, low=0, high=AT):
        rows = pl.ds(pl.multiple_of(first, 128), count)

        def one(a, carry):
            total = None
            for k in range(KT):
                term = jnp.dot(
                    lhs[step, rows, k * TILE : (k + 1) * TILE],
                    tiles[table_s[0, a * KT + k]],
                    preferred_element_type=jnp.float32,
                )
                total = term if total is None else total + term
            part[step, rows, pl.ds(pl.multiple_of(a * TILE, TILE), TILE)] = total
            return carry

        lax.fori_loop(low, high, one, 0)

    def encode(values, message):
        top = functools.reduce(jnp.maximum, [jnp.abs(v) for v in values])
        top = jnp.maximum(jnp.max(top, axis=1, keepdims=True), 1e-30)
        code = jnp.ceil(jnp.log2(top) * OCTAVE)
        factor = jnp.exp2(code * (-1.0 / OCTAVE)) * TOP
        for c, v in enumerate(values):
            message[c] = jnp.round(v * factor).astype(jnp.int32).astype(jnp.int16)
        message[len(values)] = jnp.broadcast_to(code, (8, 128)).astype(jnp.int32).astype(jnp.int16)

    def decode(message, n):
        def wide_of(c):
            return message[c].astype(jnp.int32).astype(jnp.float32)

        scale = jnp.exp2(wide_of(n) * (1.0 / OCTAVE)) * (1.0 / TOP)
        return [wide_of(c) * scale for c in range(n)]

    def rows_of(u, xd, i):
        return pl.ds(pl.multiple_of(u * 64 + xd * 16 + i * 8, 8), 8)

    def values_of(step, u, xd, first, last):
        return [part[step, rows_of(u, xd, i), c * 128 : (c + 1) * 128] for i in range(2) for c in range(first, last)]

    def add_into(step, u, xd, added):
        total = [v + w for v, w in zip(values_of(step, u, xd, 0, LANES), added)]
        for n, v in enumerate(total):
            part[step, rows_of(u, xd, n // LANES), n % LANES * 128 : (n % LANES + 1) * 128] = v
        return total

    def half_copy(step, u, way):
        return pltpu.make_async_remote_copy(
            src_ref=hs.at[step, u, way], dst_ref=hr.at[step, u, way], send_sem=h_sent,
            recv_sem=h_recv.at[step, u, way], device_id=(right, left)[way], device_id_type=MESH,
        )

    def full_copy(step, u, way):
        return pltpu.make_async_remote_copy(
            src_ref=fs.at[step, u, way], dst_ref=fr.at[step, u, way], send_sem=f_sent,
            recv_sem=f_recv.at[step, u, way], device_id=(right, left)[way], device_id_type=MESH,
        )

    def offset(zd):
        return lax.rem(z - zd + NZ + NZ // 2, NZ) - NZ // 2

    def row_copy(step, u, zd, h):
        off = offset(zd)
        slot = jnp.where(off < 0, off + 2, off + 1)
        return pltpu.make_async_remote_copy(
            src_ref=zs.at[step * UNITS + u], dst_ref=zr.at[slot, h], send_sem=z_sent, recv_sem=z_recv.at[slot, h],
            device_id=(row, zd * NX + x), device_id_type=MESH,
        )

    def collect_copy(step, u, off):
        ahead = jnp.where(off == -4, jnp.where(u % 2 == 0, 2, NZ - 2), jnp.where(off == -3, 1, NZ - 1))
        slot = jnp.where(off == -4, 1, 0)
        return pltpu.make_async_remote_copy(
            src_ref=zs.at[step * UNITS + u], dst_ref=cr.at[step, u, slot], send_sem=z_sent,
            recv_sem=c_recv.at[step, u, slot], device_id=(row, lax.rem(z + ahead, NZ) * NX + x), device_id_type=MESH,
        )

    def stage_half(step, way, first=0, count=UNITS):
        def body(n, carry):
            u = first + n
            encode(values_of(step, u, x_across, way * HALF, (way + 1) * HALF), hs.at[step, u, way])
            half_copy(step, u, way).start()
            return carry

        lax.fori_loop(0, count, body, 0)

    def stage_full(step, way, first=0):
        def body(n, carry):
            u = lax.rem(first + n, UNITS)
            arrived(hr.at[step, u, way], h_recv.at[step, u, way])
            values = values_of(step, u, x_right if way == 0 else x_left, 0, LANES)
            for n, v in enumerate(decode(hr.at[step, u, way], 2 * HALF)):
                at = n // HALF * LANES + way * HALF + n % HALF
                values[at] = values[at] + v
            encode(values, fs.at[step, u, way])
            full_copy(step, u, way).start()
            return carry

        lax.fori_loop(0, UNITS, body, 0)

    def stage_rows(step, first=0, count=UNITS):
        def body(n, carry):
            u = lax.rem(first + n, UNITS)
            zd, h = unit_of(step, u, y)
            off = offset(zd)
            for way in range(2):
                arrived(fr.at[step, u, way], f_recv.at[step, u, way])
            added = [v + w for v, w in zip(*[decode(fr.at[step, u, way], 2 * LANES) for way in range(2)])]
            encode(add_into(step, u, x, added), zs.at[step * UNITS + u])

            @pl.when((off == 1) | (off == -1))
            def _():
                row_copy(step, u, zd, h).start()

            @pl.when((off == 3) | (off < -2))
            def _():
                collect_copy(step, u, off).start()

            return carry

        lax.fori_loop(0, count, body, 0)

    def stage_collect(step, first=0):
        def body(n, carry):
            u = lax.rem(first + n, UNITS)
            zd, h = unit_of(step, u, y)
            off = offset(zd)

            def take(slot):
                arrived(cr.at[step, u, slot], c_recv.at[step, u, slot])
                return decode(cr.at[step, u, slot], 2 * LANES)

            @pl.when(jnp.where(u % 2 == 0, off == -2, off == 2))
            def _():
                add_into(step, u, x, take(1))

            @pl.when((off == 2) | (off == -2))
            def _():
                encode(add_into(step, u, x, take(0)), zs.at[step * UNITS + u])
                row_copy(step, u, zd, h).start()

            return carry

        lax.fori_loop(0, UNITS, body, 0)

    multiply(0, core * 128, 128, 0, 4)
    stage_half(0, 0, core * 2, 2)
    multiply(0, core * 128, 128, 4, 8)
    stage_half(0, 1, core * 2, 2)
    arrived(own_block(1 - core), ag_recv.at[0, 1 - core, 0])
    multiply(0, 128 - core * 128, 128, 0, 4)
    stage_half(0, 0, 2 - core * 2, 2)
    multiply(0, 128 - core * 128, 128, 4, 8)
    stage_half(0, 1, 2 - core * 2, 2)
    pass_on(1, 0, 0)
    pass_on(3, 0, 0)
    pass_on(1, 0, 1)
    pass_on(3, 0, 1)
    to_neighbours(1, 1)
    stage_full(0, 0, core * 2)
    stage_full(0, 1, core * 2)

    pass_on(1, 1, 0)
    pass_on(3, 1, 0)
    from_partner(1, 0)
    from_partner(3, 0)
    multiply(1, low=0, high=4)
    stage_half(1, 0)
    multiply(1, low=4, high=8)
    stage_half(1, 1)
    pass_on(2, 0, 0)
    pass_on(2, 0, 1)
    stage_rows(0, core * 2)
    pass_on(1, 1, 1)
    pass_on(3, 1, 1)
    stage_full(1, 0)
    stage_full(1, 1)

    from_partner(1, 1)
    from_partner(2, 0)
    multiply(2, low=0, high=4)
    stage_half(2, 0)
    pass_on(2, 1, 0)
    pass_on(2, 1, 1)
    multiply(2, low=4, high=8)
    stage_half(2, 1)
    stage_collect(0, core * 2)

    from_partner(3, 1)
    from_partner(2, 1)
    multiply(3, low=4, high=8)
    stage_half(3, 1)
    stage_full(2, 0)
    stage_full(2, 1)
    stage_rows(1)
    multiply(3, low=0, high=4)
    stage_half(3, 0)
    stage_full(3, 1)
    stage_collect(1)
    stage_full(3, 0)
    stage_rows(2)
    stage_rows(3)
    stage_collect(2)
    stage_collect(3)

    up, mine_core = lax.rem(z // 2 - y + NY, NY), z % 2
    for h in range(2):
        places = [place(delta, mine_core, h) for delta in range(NY)]
        step, u = places[0]
        for delta in range(1, NY):
            step = jnp.where(up == delta, places[delta][0], step)
            u = jnp.where(up == delta, places[delta][1], u)
        total = values_of(step, u, x, 0, LANES)
        for source in range(4):
            arrived(zr.at[source, h], z_recv.at[source, h])
            total = [v + w for v, w in zip(total, decode(zr.at[source, h], 2 * LANES))]
        for n, v in enumerate(total):
            i, c = n // LANES, n % LANES
            wide[c % 2, pl.ds((h * 16 + i * 8) * AT + c // 2, 8, stride=AT), :] = v
    for side in range(2):
        rows = wide[side, pl.ds(0, 32 * AT), :].reshape(32, AT, 128)
        out_ref[:, :, side * 128 : (side + 1) * 128] = rows.astype(jnp.bfloat16)

    def all_sent(ref, sem):
        pltpu.make_async_remote_copy(
            src_ref=ref, dst_ref=ref, send_sem=sem, recv_sem=z_recv.at[0, 0], device_id=partner, device_id_type=MESH
        ).wait_send()

    all_sent(own_block(core), block_sent)
    all_sent(lhs.at[pl.ds(0, 3)], rows_sent)
    all_sent(hs, h_sent)
    all_sent(fs, f_sent)
    all_sent(zs.at[pl.ds(0, STEPS * UNITS - 2)], z_sent)


def shards(amps, ints, task_cd, task_ab, task_count):
    smem = pl.BlockSpec(memory_space=pltpu.SMEM)
    vmem = pl.BlockSpec(memory_space=pltpu.VMEM)
    dma = pltpu.SemaphoreType.DMA

    def message(*shape):
        return pltpu.VMEM((*shape, 8, 128), jnp.int16)

    return pl.pallas_call(
        kernel,
        out_shape=jax.ShapeDtypeStruct((32, AT, TILE), jnp.bfloat16),
        in_specs=[pl.BlockSpec(memory_space=pl.ANY), pl.BlockSpec(memory_space=pl.ANY), smem, smem, smem],
        out_specs=vmem,
        scratch_shapes=[
            pltpu.VMEM((KT * AT + 1, TILE, TILE), jnp.bfloat16),
            pltpu.VMEM((128, KT, TILE), jnp.bfloat16),
            pltpu.VMEM((2, 128 * KT, 128), jnp.float32),
            pltpu.VMEM((8, 128), jnp.int32),
            pltpu.SMEM((8, 128), jnp.int32),
            pltpu.VMEM((STEPS, 64 * UNITS, KT * TILE), jnp.bfloat16),
            pltpu.VMEM((STEPS, 64 * UNITS, WIDE), jnp.float32),
            message(STEPS, UNITS, 2, HALF_MSG), message(STEPS, UNITS, 2, HALF_MSG),
            message(STEPS, UNITS, 2, ROW_MSG), message(STEPS, UNITS, 2, ROW_MSG),
            message(STEPS * UNITS, ROW_MSG), message(STEPS, UNITS, 2, ROW_MSG), message(4, 2, ROW_MSG),
            dma, dma((LOADS,)), dma, dma, dma, dma, dma, dma,
            dma((STEPS, UNITS, 2)), dma((STEPS, UNITS, 2)), dma((STEPS, UNITS, 2)), dma((STEPS, UNITS, 2)), dma((4, 2)),
        ],
        compiler_params=pltpu.CompilerParams(
            collective_id=0, has_side_effects=True, vmem_limit_bytes=60 * 1024 * 1024
        ),
    )(amps, ints, task_cd, task_ab, task_count)


def solution(mesh):
    in_specs = (P("row", "col", None), P(("row", "col"), None, None)) + (P(("row", "col")),) * 3
    return jax.shard_map(
        shards, mesh=mesh, in_specs=in_specs, out_specs=P("col", "row", None), check_vma=False
    )
```
